32 devices in a mesh: va: 2 (over y), vb: 2 (over x), oj: 8 (over z, core).
Axes of the slice: x: 2, y: 2, z: 4, core: 2. Of those that a mesh axis runs over, the one named last changes fastest.
Arguments:
- occ_slab: bfloat16 [3584, 2, 2048], P(('vb', 'oj'), None, 'va'), may hold values from -0.875 to 0.875
- pair_slab: bfloat16 [3584, 8, 2048], P(('va', 'oj'), None, 'vb'), may hold values from -0.875 to 0.875
- occ_energy: float32 [2], replicated, may hold values from -1.5 to -0.3
- pair_energy: float32 [8], P('oj'), may hold values from -1.5 to -0.3
- vir_energy: float32 [2048], replicated, may hold values from 0.2 to 3
Outputs:
- gamma_occ: float32 [3584, 2, 2048], P(('vb', 'oj'), None, 'va')
- gamma_pair: float32 [3584, 8, 2048], P('va', 'oj', 'vb')
The draws below stay inside these ranges and needn't reach their ends.
All inputs are finite; a program needn't handle non-finite values.
Results may differ from the reference program's by a relative error of at most 0.002.
Values may be sent and summed in bfloat16 or wider, within the bound.
No kernel may reach another device: no remote copies, remote signals or barrier semaphores. Data moves between devices by JAX's collectives and lax.ppermute only.
A program may use at most 192 MiB of HBM per device.

```python
import math
import jax
import jax.numpy as jnp
from jax import lax

V = 2048
NAUX = 3584
NI = 2
NJ = 8


def steps_of(own_key, shape, pieces, least, top_value):
    def one(axis_at, parts):
        steps = jax.random.uniform(jax.random.fold_in(jax.random.fold_in(own_key, 6), axis_at), (parts,), jnp.float32, least / len(pieces), top_value / len(pieces))
        return jnp.repeat(jnp.exp(steps), shape[axis_at] // parts).reshape((-1,) + (1,) * (len(shape) - axis_at - 1))

    gain = one(*pieces[0])
    for cut in pieces[1:]:
        gain = gain * one(*cut)
    return gain


def normal_values(own_key, shape, spread, bound, pieces=(), held_as=jnp.bfloat16):
    gain = steps_of(own_key, shape, pieces, -0.22, 0.18) if pieces else 1.0
    values = jax.random.normal(own_key, shape, jnp.float32) * spread * gain
    return jnp.minimum(jnp.maximum(values, -bound), bound).astype(held_as)


def setup_inputs(seed: int = 0) -> dict:
    streams_of = jax.random.split(jax.random.key(seed), 6)
    occ_slab = normal_values(streams_of[0], (NAUX, NI, V), (1.5 * (NJ * V) ** -0.333), 0.875, ((0, 16), (2, 2)))
    pair_slab = normal_values(streams_of[1], (NAUX, NJ, V), (1.5 * (NJ * V) ** -0.333), 0.875, ((0, 16), (2, 2)))
    occ_energy = jnp.clip(jax.random.uniform(streams_of[2], (NI,), jnp.float32, -1.5, -0.3), -1.5, -0.3)
    pair_energy = jnp.clip(-1.5 + 1.2 * jax.random.uniform(streams_of[3], (NJ,), jnp.float32) ** steps_of(streams_of[3], (NJ,), ((0, 8),), -0.2, 0.2), -1.5, -0.3)
    vir_energy = jnp.clip(jnp.exp(jax.random.uniform(streams_of[4], (V,), jnp.float32, math.log(0.2), math.log(3.0))), 0.2, 3.0)
    return {"occ_slab": occ_slab, "pair_slab": pair_slab, "occ_energy": occ_energy, "pair_energy": pair_energy, "vir_energy": vir_energy}


def reference(occ_slab, pair_slab, occ_energy, pair_energy, vir_energy):
    occ_wide = occ_slab.astype(jnp.float32)

    def one_pair(running, index):
        pair_rows = lax.dynamic_index_in_dim(pair_slab, index, 1, keepdims=False).astype(jnp.float32)
        pair_ints = jnp.einsum('qia,qb->iab', occ_wide, pair_rows)
        energy_j = lax.dynamic_index_in_dim(pair_energy, index, 0, keepdims=False)
        denominator = ((occ_energy[:, None, None] + energy_j) - vir_energy[None, :, None]) - vir_energy[None, None, :]
        amplitudes = (pair_ints / denominator).astype(jnp.bfloat16).astype(jnp.float32)
        gamma_part = jnp.einsum('iab,qb->qia', amplitudes, pair_rows)
        gamma_column = jnp.einsum('iab,qia->qb', amplitudes, occ_wide)
        return running + gamma_part, gamma_column

    initial = jnp.zeros((NAUX, NI, V), jnp.float32)
    gamma_occ, columns = lax.scan(one_pair, initial, jnp.arange(NJ, dtype=jnp.int32))
    gamma_pair = jnp.transpose(columns, (1, 0, 2))
    return gamma_occ, gamma_pair
```

```python
import functools

import jax
import jax.numpy as jnp
from jax import lax
from jax.experimental import pallas as pl
from jax.experimental.pallas import tpu as pltpu
from jax.sharding import PartitionSpec as P


CORES = 2
WIRE = jnp.bfloat16
F32 = jnp.float32
SAME, CORE, INNER, PLACE = 0, 1, 2, 3
ANY = pl.BlockSpec(memory_space=pl.ANY)


def gathered(occ_slab, pair_slab, occ_energy, pair_energy, vir_energy):
    occ_full = lax.all_gather(occ_slab, ("vb", "oj"), axis=0, tiled=True)
    owner_rows = lax.all_to_all(pair_slab, "oj", split_axis=1, concat_axis=0, tiled=True)
    pair_full = lax.all_gather(owner_rows, "va", axis=0, tiled=True)
    denominator = denominators(occ_energy, pair_energy, vir_energy, occ_full.shape[2], pair_full.shape[2])
    pair_ints = jnp.einsum("qia,qjb->ijab", occ_full, pair_full, preferred_element_type=F32)
    amplitudes = (pair_ints / denominator[:, None]).astype(jnp.bfloat16)
    gamma_occ = lax.psum_scatter(
        jnp.einsum("ijab,qjb->qia", amplitudes, pair_full, preferred_element_type=F32),
        ("vb", "oj"),
        scatter_dimension=0,
        tiled=True,
    )
    gamma_pair = lax.psum_scatter(
        jnp.einsum("ijab,qia->qjb", amplitudes, occ_full, preferred_element_type=F32),
        "va",
        scatter_dimension=0,
        tiled=True,
    )
    return (gamma_occ, gamma_pair)


def denominators(occ_energy, pair_energy, vir_energy, width_a, width_b):
    energy_a = lax.dynamic_slice_in_dim(vir_energy, lax.axis_index("va") * width_a, width_a)
    energy_b = lax.dynamic_slice_in_dim(vir_energy, lax.axis_index("vb") * width_b, width_b)
    return (occ_energy[:, None, None] + pair_energy[0]) - energy_a[None, :, None] - energy_b[None, None, :]


def swap(value, axis, size, offset):
    return lax.ppermute(value, axis, [(i, i ^ offset) for i in range(size)])


def params():
    return pltpu.CompilerParams(vmem_limit_bytes=56 * 2**20)


def cost(flops, *arrays):
    moved = sum(v.size * v.dtype.itemsize for v in arrays)
    return pl.CostEstimate(flops=flops, bytes_accessed=moved, transcendentals=0)


def copy_either(first, a, b, target, sem):
    @pl.when(first)
    def _():
        pltpu.make_async_copy(a, target, sem).start()

    @pl.when(jnp.logical_not(first))
    def _():
        pltpu.make_async_copy(b, target, sem).start()


def contract_kernel(places, rows, tile, final, flags, *refs):
    slots = len(places)
    occ = [refs[4 * s : 4 * s + 4] for s in range(slots)]
    refs = refs[4 * slots :]
    pairs = []
    for place in places:
        pairs.append([refs[4 * n : 4 * n + 4] for n in range(len(place))])
        refs = refs[4 * len(place) :]
    acc = None
    if places[0] != (0,):
        acc, refs = refs[0], refs[1:]
    if final:
        (energy_ij, energy_a, energy_b), refs = refs[:3], refs[3:]
    out, occ_v, pair_v, sem = refs
    i, t = pl.program_id(0), pl.program_id(1)
    core, same, inner = flags[CORE], flags[SAME] == 1, flags[INNER] == 1

    @pl.when((i == 0) & (t == 0))
    def _():
        for s in range(slots):
            for k in range(4):
                at = pl.ds((4 * s + k) * rows, rows)
                use_z = same if k % 2 == 0 else jnp.logical_not(same)
                choices = [(p[(k // 2) * 2], p[(k // 2) * 2 + 1]) for p in pairs[s]]
                target = pair_v.at[at]
                if len(choices) == 1:
                    copy_either(use_z, choices[0][0].at[core], choices[0][1].at[core], target, sem.at[0])
                else:
                    for flag, (z_ref, y_ref) in ((inner, choices[1]), (jnp.logical_not(inner), choices[0])):
                        @pl.when(flag)
                        def _(z_ref=z_ref, y_ref=y_ref, target=target, use_z=use_z):
                            copy_either(use_z, z_ref.at[core], y_ref.at[core], target, sem.at[0])
                pltpu.make_async_copy(occ[s][k].at[0], occ_v.at[0, at], sem.at[1]).start()
        for s in range(slots):
            for k in range(4):
                at = pl.ds((4 * s + k) * rows, rows)
                pltpu.make_async_copy(occ[s][k].at[1], occ_v.at[1, at], sem.at[2]).start()
        pltpu.make_async_copy(pair_v, pair_v, sem.at[0]).wait()
        pltpu.make_async_copy(occ_v.at[0], occ_v.at[0], sem.at[1]).wait()

    @pl.when((i == 1) & (t == 0))
    def _():
        pltpu.make_async_copy(occ_v.at[1], occ_v.at[1], sem.at[2]).wait()

    block = pair_v[:, pl.ds(pl.multiple_of(t * tile, tile), tile)]
    part = lax.dot_general(block, occ_v[i], (((0,), (0,)), ((), ())), preferred_element_type=F32)
    if acc is not None:
        part = acc[0] + part
    if final:
        part = part / ((energy_ij[i] - energy_a[...]) - energy_b[...])
    out[0] = part.astype(out.dtype)


def contract(places, flags, occ, pairs, acc, energies):
    rows, width_a, width_b = occ[0][0].shape[1], occ[0][0].shape[2], pairs[0][0][0].shape[2]
    tile = width_b // 2
    depth = 4 * len(places) * rows
    count = occ[0][0].shape[0]
    final = energies is not None
    block = pl.BlockSpec((1, tile, width_a), lambda i, t, *_: (i, t, 0))
    flat = [v for s in occ for v in s] + [v for s in pairs for p in s for v in p]
    specs = [ANY] * len(flat)
    if acc is not None:
        flat.append(acc)
        specs.append(block)
    if final:
        flat += energies
        specs += [
            pl.BlockSpec(memory_space=pltpu.SMEM),
            pl.BlockSpec((1, width_a), lambda i, t, *_: (0, 0)),
            pl.BlockSpec((tile, 1), lambda i, t, *_: (t, 0)),
        ]
    out = jax.ShapeDtypeStruct((count, width_b, width_a), jnp.bfloat16 if final else F32)
    return pl.pallas_call(
        functools.partial(contract_kernel, places, rows, tile, final),
        grid_spec=pltpu.PrefetchScalarGridSpec(
            num_scalar_prefetch=1,
            grid=(count, width_b // tile),
            in_specs=specs,
            out_specs=block,
            scratch_shapes=[
                pltpu.VMEM((count, depth, width_a), jnp.bfloat16),
                pltpu.VMEM((depth, width_b), jnp.bfloat16),
                pltpu.SemaphoreType.DMA((3,)),
            ],
        ),
        out_shape=out,
        compiler_params=params(),
        cost_estimate=cost(2 * count * depth * width_a * width_b, out),
        name="contract",
    )(flags, *flat)


def pair_kernel(low, high, own, flags, *refs):
    occ, (amps, out, occ_v, amps_v, sem) = refs[:16], refs[16:]
    g = pl.program_id(0)
    count = high - low
    same = flags[SAME] == 1

    @pl.when(g == 0)
    def _():
        pltpu.make_async_copy(amps, amps_v, sem.at[count]).start()
        for slot in range(4):
            for parity in range(2):
                at = flags[PLACE + 2 * slot + parity] - low
                use_z = same if own else jnp.logical_not(same)

                @pl.when((at >= 0) & (at < count))
                def _(slot=slot, parity=parity, at=at, use_z=use_z):
                    z_ref, x_ref = occ[4 * slot + 2 * parity], occ[4 * slot + 2 * parity + 1]
                    copy_either(use_z, z_ref, x_ref, occ_v.at[at], sem.at[at])

        pltpu.make_async_copy(amps, amps_v, sem.at[count]).wait()

    pltpu.make_async_copy(occ_v.at[g], occ_v.at[g], sem.at[g]).wait()
    total = None
    for i in range(occ_v.shape[1]):
        part = lax.dot_general(occ_v[g, i], amps_v[i], (((1,), (1,)), ((), ())), preferred_element_type=F32)
        total = part if total is None else total + part
    out[...] = total.astype(out.dtype)


def pair_rows(low, high, own, flags, occ, amps, dtype):
    flat = [v for s in occ for v in s]
    count, rows, width_a = flat[0].shape
    width_b = amps.shape[1]
    out = jax.ShapeDtypeStruct(((high - low) * rows, width_b), dtype)
    return pl.pallas_call(
        functools.partial(pair_kernel, low, high, own),
        grid_spec=pltpu.PrefetchScalarGridSpec(
            num_scalar_prefetch=1,
            grid=(high - low,),
            in_specs=[ANY] * 17,
            out_specs=pl.BlockSpec((rows, width_b), lambda g, *_: (g, 0)),
            scratch_shapes=[
                pltpu.VMEM((high - low, count, rows, width_a), jnp.bfloat16),
                pltpu.VMEM(amps.shape, jnp.bfloat16),
                pltpu.SemaphoreType.DMA((high - low + 1,)),
            ],
        ),
        out_shape=out,
        compiler_params=params(),
        cost_estimate=cost(2 * out.size * count * width_a, out, amps),
        name="pair_rows",
    )(flags, *flat, amps)


def occ_kernel(n, own, flags, *refs):
    pairs, (amps, amps_other), refs = refs[: 2 * n], refs[2 * n : 2 * n + 2], refs[2 * n + 2 :]
    outs, (pair_v, amps_v, sem) = refs[:n], refs[n:]
    g = pl.program_id(0)
    same, core = flags[SAME] == 1, flags[CORE]

    @pl.when(g == 0)
    def _():
        for k, v in enumerate((amps, amps_other)):
            pltpu.make_async_copy(v, amps_v.at[k], sem.at[n + k]).start()
        for k in range(n):
            use_z = same if own else jnp.logical_not(same)
            copy_either(use_z, pairs[2 * k], pairs[2 * k + 1], pair_v.at[k], sem.at[k])
        for k in range(2):
            pltpu.make_async_copy(amps, amps_v.at[k], sem.at[n + k]).wait()

    pltpu.make_async_copy(pair_v.at[g], pair_v.at[g], sem.at[g]).wait()
    mine, theirs = pair_v[g, core], pair_v[g, 1 - core]
    for i in range(amps_v.shape[1]):
        total = jnp.dot(mine, amps_v[0, i], preferred_element_type=F32)
        total += jnp.dot(theirs, amps_v[1, i], preferred_element_type=F32)
        total = total.astype(outs[0].dtype)
        for k in range(n):
            @pl.when(g == k)
            def _(k=k, i=i, total=total):
                outs[k][i] = total


def occ_rows(own, flags, pairs, amps, amps_other, dtype):
    n = len(pairs)
    flat = [v for p in pairs for v in p]
    both, rows, width_b = flat[0].shape
    count, _, width_a = amps.shape
    out = jax.ShapeDtypeStruct((count, rows, width_a), dtype)
    return pl.pallas_call(
        functools.partial(occ_kernel, n, own),
        grid_spec=pltpu.PrefetchScalarGridSpec(
            num_scalar_prefetch=1,
            grid=(n,),
            in_specs=[ANY] * (2 * n + 2),
            out_specs=[pl.BlockSpec(out.shape, lambda g, *_: (0, 0, 0))] * n,
            scratch_shapes=[
                pltpu.VMEM((n, both, rows, width_b), jnp.bfloat16),
                pltpu.VMEM((both,) + amps.shape, jnp.bfloat16),
                pltpu.SemaphoreType.DMA((n + 2,)),
            ],
        ),
        out_shape=[out] * n,
        compiler_params=params(),
        cost_estimate=cost(2 * n * out.size * both * width_b, amps, amps, *[out] * n),
        name="occ_rows",
    )(flags, *flat, amps, amps_other)


def exchanged(ring, chips, occ_slab, pair_slab, occ_energy, pair_energy, vir_energy):
    x, y, o = lax.axis_index("vb"), lax.axis_index("va"), lax.axis_index("oj")
    z, core = o // CORES, o % CORES
    inside = jnp.logical_and(z > 0, z < chips - 1)
    inner = inside.astype(jnp.int32)
    rows, width_a, width_b = occ_slab.shape[0], occ_slab.shape[2], pair_slab.shape[2]
    near_far = [jnp.int32(0), jnp.int32(1), 2 + inner, 3 - inner]
    places = [o ^ (CORES * m + p) for m in near_far for p in range(CORES)]
    flags = jnp.stack([(x == y).astype(jnp.int32), core, inner] + places)

    def along_core(v):
        return swap(v, "oj", ring, 1)

    def along_z(v, m):
        return swap(v, "oj", ring, m * CORES)

    def some_z(v, line):
        return lax.ppermute(v, "oj", [(c * CORES + k, d * CORES + k) for c, d in line for k in range(CORES)])

    occ_own = jnp.transpose(occ_slab, (1, 0, 2))
    pair_by_j = lax.optimization_barrier(jnp.transpose(pair_slab, (1, 0, 2)))

    def for_chip(m):
        return lax.dynamic_slice_in_dim(pair_by_j, (z ^ m) * CORES, CORES, 0)

    pair_z = [for_chip(0)] + [along_z(for_chip(m), m) for m in (1, 2, 3)]
    pair_y = [swap(v, "va", 2, 1) for v in pair_z]
    pair_all = [(pair_z[m], pair_y[m], along_core(pair_z[m]), along_core(pair_y[m])) for m in range(chips)]

    occ_near = along_z(occ_own, 1)
    cross = [some_z(v, ((1, 2), (2, 1))) for v in (occ_own, occ_near)]
    relay = [some_z(v, ((1, 0), (2, 3))) for v in cross]
    far = [jnp.where(inside, c, r) for c, r in zip(cross, relay)]
    occ_z = [occ_own, occ_near] + far
    occ_x = [swap(v, "vb", 2, 1) for v in occ_z]
    occ_all = [(occ_z[s], occ_x[s], along_core(occ_z[s]), along_core(occ_x[s])) for s in range(chips)]

    energies = [
        occ_energy + pair_energy[0],
        lax.dynamic_slice_in_dim(vir_energy, y * width_a, width_a)[None, :],
        lax.dynamic_slice_in_dim(vir_energy, x * width_b, width_b)[:, None],
    ]
    far_pairs = [pair_all[2], pair_all[3]]
    acc = contract(((0,), (1,)), flags, occ_all[:2], [[pair_all[0]], [pair_all[1]]], None, None)
    acc = contract(((2, 3),), flags, occ_all[2:3], [far_pairs], acc, None)
    amps = contract(((2, 3),), flags, occ_all[3:4], [far_pairs[::-1]], acc, energies)
    amps_other = along_core(amps)

    blocks = ring // 2
    arrived = []
    for low in (0, blocks):
        leave = pair_rows(low, low + blocks, False, flags, occ_all, amps, WIRE)
        arrived.append(swap(leave, "va", 2, 1))
    keep = pair_rows(0, ring, True, flags, occ_all, amps, F32)
    gamma_pair = keep + jnp.concatenate(arrived).astype(F32)
    gamma_pair = gamma_pair[:, None, :]

    choices = [(pair_z[m], pair_y[m]) for m in range(chips)]
    got = [None] * chips
    for m in (3, 1):
        first, second = occ_rows(False, flags, [choices[m], choices[m - 1]], amps, amps_other, WIRE)
        got[m], got[m - 1] = swap(first, "vb", 2, 1), swap(second, "vb", 2, 1)
    here = occ_rows(True, flags, choices, amps, amps_other, F32)
    here = [h + g.astype(F32) for h, g in zip(here, got)]
    gamma_occ = here[0]
    for m in (3, 2, 1):
        gamma_occ = gamma_occ + along_z(here[m].astype(WIRE), m).astype(F32)
    return (jnp.transpose(gamma_occ, (1, 0, 2)), gamma_pair)


def solution(mesh):
    sizes = mesh.shape
    ring = sizes["oj"]
    chips = ring // CORES
    placed = (P(("vb", "oj"), None, "va"), P(("va", "oj"), None, "vb"), P(), P("oj"), P())
    if sizes["va"] == 2 and sizes["vb"] == 2 and chips == 4:
        def per_device(*args):
            return exchanged(ring, chips, *args)
    else:
        per_device = gathered
    return jax.shard_map(
        per_device,
        mesh=mesh,
        in_specs=placed,
        out_specs=(P(("vb", "oj"), None, "va"), P("va", "oj", "vb")),
        check_vma=False,
    )
```
